32 devices in a mesh: dp: 8 (over y, x, core), ctx: 4 (over z).
Axes of the slice: x: 2, y: 2, z: 4, core: 2. Of those that a mesh axis runs over, the one named last changes fastest.
Arguments:
- tokens: bfloat16 [1024, 16, 768], P('ctx', 'dp'), may hold values from -6 to 6
- lengths: int32 [16], P('dp'), may hold values from 256 to 1024, as said below
- teacher: bfloat16 [1024, 16, 768], P('ctx', 'dp'), may hold values from -12 to 12
- query_weight: bfloat16 [768, 768], P(('dp', 'ctx')), may hold values from -0.3125 to 0.3125
- query_bias: bfloat16 [768], P(('dp', 'ctx')), may hold values from -1.1953125 to 1.1953125
- key_weight: bfloat16 [768, 768], P(('dp', 'ctx')), may hold values from -0.21875 to 0.21875
- value_weight: bfloat16 [768, 768], P(('dp', 'ctx')), may hold values from -0.21875 to 0.21875
- value_bias: bfloat16 [768], P(('dp', 'ctx')), may hold values from -1.1953125 to 1.1953125
- out_weight: bfloat16 [768, 768], P(('dp', 'ctx')), may hold values from -0.875 to 0.875
- out_bias: bfloat16 [768], P(('dp', 'ctx')), may hold values from -1.1953125 to 1.1953125
- first_gain: bfloat16 [768], P(('dp', 'ctx')), may hold values from 0.5 to 1.5
- first_shift: bfloat16 [768], P(('dp', 'ctx')), may hold values from -1.1953125 to 1.1953125
- up_weight: bfloat16 [768, 3072], P(('dp', 'ctx')), may hold values from -0.21875 to 0.21875
- up_bias: bfloat16 [3072], P(('dp', 'ctx')), may hold values from -1.1953125 to 1.1953125
- down_weight: bfloat16 [3072, 768], P(('dp', 'ctx')), may hold values from -0.109375 to 0.109375
- down_bias: bfloat16 [768], P(('dp', 'ctx')), may hold values from -1.1953125 to 1.1953125
- second_gain: bfloat16 [768], P(('dp', 'ctx')), may hold values from 0.5 to 1.5
- second_shift: bfloat16 [768], P(('dp', 'ctx')), may hold values from -1.1953125 to 1.1953125
Outputs:
- layer_out: bfloat16 [1024, 16, 768], P('ctx', 'dp')
- loss: float32 [], replicated
- grad_tokens: bfloat16 [1024, 16, 768], P('ctx', 'dp')
- grad_query_weight: float32 [768, 768], P(('dp', 'ctx'))
- grad_query_bias: float32 [768], P(('dp', 'ctx'))
- grad_key_weight: float32 [768, 768], P(('dp', 'ctx'))
- grad_value_weight: float32 [768, 768], P(('dp', 'ctx'))
- grad_value_bias: float32 [768], P(('dp', 'ctx'))
- grad_out_weight: float32 [768, 768], P(('dp', 'ctx'))
- grad_out_bias: float32 [768], P(('dp', 'ctx'))
- grad_first_gain: float32 [768], P(('dp', 'ctx'))
- grad_first_shift: float32 [768], P(('dp', 'ctx'))
- grad_up_weight: float32 [768, 3072], P(('dp', 'ctx'))
- grad_up_bias: float32 [3072], P(('dp', 'ctx'))
- grad_down_weight: float32 [3072, 768], P(('dp', 'ctx'))
- grad_down_bias: float32 [768], P(('dp', 'ctx'))
- grad_second_gain: float32 [768], P(('dp', 'ctx'))
- grad_second_shift: float32 [768], P(('dp', 'ctx'))
The draws below stay inside these ranges and needn't reach their ends.
Inputs may be any that keep to these rules, and one draw needn't show every extreme that they name: lengths[s] is the number of valid leading slots of sequence s; later slots are padding; some sequence has 1024 valid slots in every draw.
All inputs are finite; a program needn't handle non-finite values.
Results may differ from the reference program's by a relative error of at most 0.03.
Values may be sent and summed in bfloat16 or wider, within the bound.
No kernel may reach another device: no remote copies, remote signals or barrier semaphores. Data moves between devices by JAX's collectives and lax.ppermute only.
A program may use at most 192 MiB of HBM per device.

```python
import jax
import jax.numpy as jnp
from jax import lax

D = 768
H = 12
HD = 64
FF = 3072
LEN = 1024
SEQS = 16


def draw_lengths(key, part):
    values = jax.random.randint(key, (SEQS,), LEN // 4, LEN + 1, dtype=jnp.int32)
    return values.at[0].set(LEN)


def draw_teacher(key, part):
    place = jnp.arange(SEQS, dtype=jnp.float32) / max(SEQS - 1, 1)
    values = jnp.clip(jax.random.normal(key, (LEN, SEQS, D), jnp.float32), -6.0, 6.0)
    scale = 0.5 + 1.5 * place
    return (values * scale[None, :, None]).astype(jnp.bfloat16)


def levels(key, shape, shards, smallest, largest):
    def one(axis_at, blocks):
        draws = jax.random.uniform(jax.random.fold_in(jax.random.fold_in(key, 6), axis_at), (blocks,), jnp.float32, smallest / len(shards), largest / len(shards))
        return jnp.repeat(jnp.exp(draws), shape[axis_at] // blocks).reshape((-1,) + (1,) * (len(shape) - axis_at - 1))

    loudness = one(*shards[0])
    for cut in shards[1:]:
        loudness = loudness * one(*cut)
    return loudness


def bell_draw(stream_key, dims, scale, bound, pieces=(), kind=jnp.bfloat16):
    level = levels(stream_key, dims, pieces, -0.22, 0.18) if pieces else 1.0
    values = jax.random.normal(stream_key, dims, jnp.float32) * scale * level
    return jnp.minimum(jnp.maximum(values, -bound), bound).astype(kind)


def setup_inputs(seed: int = 0) -> dict:
    key_of = jax.random.split(jax.random.key(seed), 19)
    return {
        "tokens": bell_draw(key_of[0], (LEN, SEQS, D), 1.0, 6.0, ((0, 4), (1, 8))),
        "lengths": draw_lengths(jax.random.fold_in(key_of[18], 71), 0),
        "teacher": draw_teacher(jax.random.fold_in(key_of[18], 71), 0),
        "query_weight": bell_draw(key_of[3], (D, D), (D // 2) ** -0.5, 0.3125, ((0, 32),)),
        "query_bias": bell_draw(key_of[4], (D,), 0.2, 1.1953125, ((0, 32),)),
        "key_weight": bell_draw(key_of[5], (D, D), D ** -0.5, 0.21875, ((0, 32),)),
        "value_weight": bell_draw(key_of[6], (D, D), D ** -0.5, 0.21875, ((0, 32),)),
        "value_bias": bell_draw(key_of[7], (D,), 0.2, 1.1953125, ((0, 32),)),
        "out_weight": bell_draw(key_of[8], (D, D), (D // 16) ** -0.5, 0.875, ((0, 32),)),
        "out_bias": bell_draw(key_of[9], (D,), 0.2, 1.1953125, ((0, 32),)),
        "first_gain": jnp.clip(1.0 + 0.1 * jax.random.normal(key_of[10], (D,), jnp.float32), 0.5, 1.5).astype(jnp.bfloat16),
        "first_shift": bell_draw(key_of[11], (D,), 0.2, 1.1953125, ((0, 32),)),
        "up_weight": bell_draw(key_of[12], (D, FF), D ** -0.5, 0.21875, ((0, 32),)),
        "up_bias": bell_draw(key_of[13], (FF,), 0.2, 1.1953125, ((0, 32),)),
        "down_weight": bell_draw(key_of[14], (FF, D), FF ** -0.5, 0.109375, ((0, 32),)),
        "down_bias": bell_draw(key_of[15], (D,), 0.2, 1.1953125, ((0, 32),)),
        "second_gain": jnp.clip(1.0 + 0.1 * jax.random.normal(key_of[16], (D,), jnp.float32), 0.5, 1.5).astype(jnp.bfloat16),
        "second_shift": bell_draw(key_of[17], (D,), 0.2, 1.1953125, ((0, 32),)),
    }


@jax.custom_vjp
def low(v):
    return lax.optimization_barrier(v.astype(jnp.bfloat16)).astype(jnp.float32)

@jax.custom_vjp
def low_back(v):
    return v

def low_keep(v):
    return (low(v), None)

def low_pass(kept, grad):
    return (grad,)

def back_keep(v):
    return (v, None)

def back_low(kept, grad):
    return (low(grad),)
low.defvjp(low_keep, low_pass)
low_back.defvjp(back_keep, back_low)
EPSILON = 1e-12
MASKED = -1e+30

def exact_product(left, right):
    return jnp.dot(left, right, precision=lax.Precision.HIGHEST, preferred_element_type=jnp.float32)

def normalize(values, gain, shift):
    centre = values - lax.optimization_barrier(jnp.mean(values, axis=-1, keepdims=True))
    spread = lax.optimization_barrier(jnp.mean(centre * centre, axis=-1, keepdims=True))
    return centre * lax.rsqrt(spread + EPSILON) * gain + shift

def attend_one(inputs):
    query, keyed, valued, length = inputs
    query = query.reshape(LEN, H, HD)
    keyed = keyed.reshape(LEN, H, HD)
    valued = valued.reshape(LEN, H, HD)
    scores = jnp.einsum('qhd,khd->hqk', query, keyed, precision=lax.Precision.HIGHEST) * HD ** (-0.5)
    scores = low_back(scores)
    valid = jnp.arange(LEN) < length
    scores = jnp.where(valid[None, None, :], scores, MASKED)
    probs = low(jax.nn.softmax(scores, axis=-1))
    mixed = jnp.einsum('hqk,khd->qhd', probs, valued, precision=lax.Precision.HIGHEST)
    return mixed.reshape(LEN, D)

def apply_layer(hidden, params, lengths):
    query_weight, query_bias, key_weight, value_weight, value_bias, out_weight, out_bias, first_gain, first_shift, up_weight, up_bias, down_weight, down_bias, second_gain, second_shift = params
    flat = hidden.reshape(LEN * SEQS, D)
    flat_low = low(flat)
    query = low_back(low(exact_product(flat_low, query_weight) + query_bias))
    keyed = low_back(low(exact_product(flat_low, key_weight)))
    valued = low_back(low(exact_product(flat_low, value_weight) + value_bias))

    def by_sequence(values):
        return values.reshape(LEN, SEQS, D).transpose(1, 0, 2)
    mixed = lax.map(jax.checkpoint(attend_one), (by_sequence(query), by_sequence(keyed), by_sequence(valued), lengths))
    mixed = mixed.transpose(1, 0, 2).reshape(LEN * SEQS, D)
    mixed = low_back(low(mixed))
    branch = low_back(exact_product(mixed, out_weight) + out_bias)
    first = normalize(flat + branch, first_gain, first_shift)
    inner = low_back(exact_product(low(first), up_weight) + up_bias)
    active = low(jax.nn.gelu(inner, approximate=True))
    outer = low_back(exact_product(active, down_weight) + down_bias)
    result = normalize(first + outer, second_gain, second_shift)
    return result.reshape(LEN, SEQS, D)

def reference(tokens, lengths, teacher, query_weight, query_bias, key_weight, value_weight, value_bias, out_weight, out_bias, first_gain, first_shift, up_weight, up_bias, down_weight, down_bias, second_gain, second_shift):
    params = tuple((w.astype(jnp.float32) for w in (query_weight, query_bias, key_weight, value_weight, value_bias, out_weight, out_bias, first_gain, first_shift, up_weight, up_bias, down_weight, down_bias, second_gain, second_shift)))
    start = tokens.astype(jnp.float32)
    target = teacher.astype(jnp.float32)
    live = (jnp.arange(LEN)[:, None] < lengths[None, :]).astype(jnp.float32)

    def objective(start, params):
        hidden = apply_layer(apply_layer(start, params, lengths), params, lengths)
        diff = (hidden - target) * live[:, :, None]
        return (hidden, 0.5 * jnp.sum(diff * diff))
    (result, half), pullback = jax.vjp(objective, start, params)
    grad_start, grads = pullback((jnp.zeros_like(result), jnp.ones((), jnp.float32)))
    count = jnp.sum(live)
    loss = 2.0 * half / (count * D)
    return (result.astype(jnp.bfloat16), loss, grad_start.astype(jnp.bfloat16), grads[0], grads[1], grads[2], grads[3], grads[4], grads[5], grads[6], grads[7], grads[8], grads[9], grads[10], grads[11], grads[12], grads[13], grads[14])
```

```python
import functools

import jax
import jax.numpy as jnp
from jax import lax
from jax.experimental import pallas as pl
from jax.experimental.pallas import tpu as pltpu
from jax.sharding import PartitionSpec as P

H = 12
HD = 64
EPSILON = 1e-12
MASKED = -1e30
LOG2E = 1.4426950408889634
AXES = ("dp", "ctx")
BF = jnp.bfloat16
F32 = jnp.float32


def mm(left, right):
    return jnp.dot(left, right, preferred_element_type=F32)


def mm_rows(left, right):
    return lax.dot_general(left, right, (((0,), (0,)), ((), ())), preferred_element_type=F32)


def mm_back(left, right):
    return lax.dot_general(left, right, (((1,), (1,)), ((), ())), preferred_element_type=F32)


def normalize(values, gain, shift):
    centre = values - jnp.mean(values, axis=-1, keepdims=True)
    spread = jnp.mean(centre * centre, axis=-1, keepdims=True)
    return centre * lax.rsqrt(spread + EPSILON) * gain + shift


def activate(values):
    return jax.nn.gelu(values, approximate=True)


def column_sum(values):
    return jnp.sum(values.astype(F32), axis=0)


class Grid:
    def __init__(self, n_dp, n_ctx):
        self.n_dp, self.n_ctx, self.n = n_dp, n_ctx, n_dp * n_ctx
        self.dp, self.ctx = lax.axis_index("dp"), lax.axis_index("ctx")
        self.lin = self.dp * n_ctx + self.ctx
        self.ctx_bits = [1 << i for i in range(n_ctx.bit_length() - 1)]
        self.core_bit = n_ctx
        self.top_bits = [2 * n_ctx << i for i in range(n_dp.bit_length() - 2)]
        self.core = self.dp % 2

    def flip(self, value, mask):
        return lax.ppermute(value, AXES, [(i, i ^ mask) for i in range(self.n)])

    def bit(self, mask):
        return (self.lin // mask) % 2


def gather_ctx(grid, part):
    parts = [part]
    for mask in reversed(grid.ctx_bits):
        sent = jnp.concatenate(parts, 0) if len(parts) > 1 else parts[0]
        got = jnp.split(grid.flip(sent, mask), len(parts), 0)
        low = grid.bit(mask) == 0
        parts = [
            jnp.where(low == first, mine, other)
            for mine, other in zip(parts, got)
            for first in (True, False)
        ]
    return jnp.concatenate(parts, 0)


def gather_top(grid, part):
    width = part.shape[1]
    if len(grid.top_bits) == 2:
        a, b = grid.top_bits
        cut = width // 256 * 128
        by_a, by_b = grid.flip(part, a), grid.flip(part, b)
        left = grid.flip(by_b[:, :cut], a)
        right = grid.flip(by_a[:, cut:], b)
        pieces = [(0, 0, part), (a, 0, by_a), (b, 0, by_b), (a ^ b, 0, left), (a ^ b, cut, right)]
    else:
        pieces = [(0, 0, part)]
        for bit in grid.top_bits:
            pieces = pieces + [(m ^ bit, c, grid.flip(v, bit)) for m, c, v in pieces]
    core = grid.core_bit
    pieces = pieces + [(m ^ core, c, grid.flip(v, core)) for m, c, v in pieces]
    return [(m // grid.n_ctx, c, v) for m, c, v in pieces]


def assemble(grid, pieces, rows, targets, shapes):
    copies = []
    for number, (rel, start, value) in enumerate(pieces):
        for first, columns, array, column, height, offset in targets:
            low, high = max(first, start), min(first + columns, start + value.shape[1])
            if low < high:
                copies.append((number, rel, low - start, high - low, array, column + low - first, height, offset))

    def kernel(me, *refs):
        sources, outs, sems = refs[: len(pieces)], refs[len(pieces) : -1], refs[-1]
        started = []
        for i, (number, rel, source, columns, array, column, height, offset) in enumerate(copies):
            row = pl.multiple_of((me[0] ^ rel) * height + offset, 16)
            copy = pltpu.make_async_copy(
                sources[number].at[:, pl.ds(source, columns)],
                outs[array].at[pl.ds(row, rows), pl.ds(column, columns)],
                sems.at[i],
            )
            copy.start()
            started.append(copy)
        for copy in started:
            copy.wait()

    return pl.pallas_call(
        kernel,
        out_shape=[jax.ShapeDtypeStruct(s, BF) for s in shapes],
        grid_spec=pltpu.PrefetchScalarGridSpec(
            num_scalar_prefetch=1,
            grid=(1,),
            in_specs=[pl.BlockSpec(memory_space=pl.ANY)] * len(pieces),
            out_specs=[pl.BlockSpec(memory_space=pltpu.VMEM)] * len(shapes),
            scratch_shapes=[pltpu.SemaphoreType.DMA((len(copies),))],
        ),
        name="assemble",
    )(grid.dp.reshape(1), *[v for _, _, v in pieces])


def scatter_sum(grid, total):
    rows, width = total.shape
    block = rows // grid.n_dp
    top = grid.n_dp // 2
    pick = functools.partial(lax.dynamic_index_in_dim, keepdims=False)
    value = total.reshape(top, 2, block, width)
    got = grid.flip(pick(value, 1 - grid.core, 1).astype(BF), grid.core_bit)
    value = pick(value, grid.core, 1) + got.astype(F32)

    def step(value, mask, axis):
        bit = grid.bit(mask)
        got = grid.flip(pick(value, 1 - bit, axis).astype(BF), mask)
        return pick(value, bit, axis) + got.astype(F32)

    if len(grid.top_bits) == 2:
        a, b = grid.top_bits
        cut = width // 256 * 128
        value = value.reshape(2, 2, block, width)
        left, right = value[..., :cut], value[..., cut:]
        left = step(step(left, a, 1), b, 0)
        right = step(step(right, b, 0), a, 0)
        value = jnp.concatenate([left, right], -1)
    else:
        for mask in reversed(grid.top_bits):
            value = step(value.reshape(2, value.shape[0] // 2, block, width), mask, 0)
        value = value[0]
    own = block // grid.n_ctx
    for mask in grid.ctx_bits:
        value = step(value.reshape(-1, 2, own, width), mask, 1)
        value = value.reshape(-1, width)
    return value


def lanes(shape):
    return lax.broadcasted_iota(jnp.int32, shape, len(shape) - 1)


def attend_kernel(count, scale, q_ref, mask_ref, *refs):
    k_refs, v_refs = refs[:count], refs[count : 2 * count]
    o_ref, lse_ref = refs[2 * count :]
    rows = q_ref.shape[0]
    factor = scale * LOG2E
    lane = lanes((rows, 128))
    first = lane < HD
    one = jnp.where(lane % HD == 0, 1.0, 0.0).astype(BF)
    outs = []
    for head in range(2):
        keep = first if head == 0 else jnp.logical_not(first)
        query = jnp.where(keep, q_ref[...], one)
        scores = [
            mm_back(jnp.where(keep, k_refs[i][...], mask_ref[i]), query) for i in range(count)
        ]
        top = functools.reduce(jnp.maximum, [jnp.max(s, axis=0, keepdims=True) for s in scores])
        top = top * factor
        mixed = None
        for i in range(count):
            probs = jnp.exp2(scores[i] * factor - top).astype(BF)
            value = jnp.where(keep, v_refs[i][...], jnp.ones((), BF))
            part = mm_rows(value, probs)
            mixed = part if mixed is None else mixed + part
        if head == 0:
            total, mixed = mixed[HD : HD + 1], mixed[:HD]
        else:
            total, mixed = mixed[:1], mixed[HD:]
        outs.append(mixed / total)
        lse_ref[0, head : head + 1, :] = top + jnp.log2(total)
    o_ref[...] = jnp.concatenate(outs, 0).T.astype(BF)


def attend(query, keyed, mask):
    rows, model = query.shape
    count, pairs = len(keyed), model // 128
    at = lambda base: pl.BlockSpec((rows, 128), lambda j: (0, base + j))
    return pl.pallas_call(
        functools.partial(attend_kernel, count, HD**-0.5),
        grid=(pairs,),
        in_specs=[at(0), pl.BlockSpec((count, rows, 128), lambda j: (0, 0, 0))]
        + [at(0)] * count
        + [at(pairs)] * count,
        out_specs=[at(0), pl.BlockSpec((1, 8, rows), lambda j: (j, 0, 0))],
        out_shape=[
            jax.ShapeDtypeStruct((rows, model), BF),
            jax.ShapeDtypeStruct((pairs, 8, rows), F32),
        ],
        compiler_params=pltpu.CompilerParams(vmem_limit_bytes=56 << 20),
        name="attend",
    )(query, mask, *keyed, *keyed)


def attend_back_kernel(count, scale, q_ref, do_ref, o_ref, lse_ref, mask_ref, *refs):
    k_refs, v_refs = refs[:count], refs[count : 2 * count]
    dq_ref = refs[2 * count]
    dk_refs, dv_refs = refs[2 * count + 1 : 3 * count + 1], refs[3 * count + 1 :]
    rows = q_ref.shape[0]
    factor = scale * LOG2E
    lane = lanes((rows, 128))
    first = lane < HD
    one = jnp.where(lane % HD == 0, 1.0, 0.0).astype(BF)
    two = jnp.where(lane % HD < 2, 1.0, 0.0).astype(BF)
    wide = do_ref[...].astype(F32)
    product = wide * o_ref[...].astype(F32)
    d_query = []
    keeps = (first, jnp.logical_not(first))
    d_key = [[None] * 2 for _ in range(count)]
    d_value = [[None] * 2 for _ in range(count)]
    for head in range(2):
        keep = keeps[head]
        query = jnp.where(keep, q_ref[...], one)
        delta = jnp.sum(jnp.where(keep, product, 0.0), axis=1, keepdims=True)
        high = delta.astype(BF).astype(F32)
        spare = lane % HD
        extra = jnp.where(spare == 0, -high, jnp.where(spare == 1, high - delta, 0.0))
        d_out = jnp.where(keep, wide, extra).astype(BF)
        lse = lse_ref[0, head : head + 1, :]
        grad = None
        for i in range(count):
            key = jnp.where(keep, k_refs[i][...], mask_ref[i])
            scores = mm_back(key, query)
            probs = jnp.exp2(scores * factor - lse)
            d_probs = mm_back(jnp.where(keep, v_refs[i][...], two), d_out)
            d_scores = (probs * d_probs).astype(BF)
            d_value[i][head] = mm(probs.astype(BF), do_ref[...])
            d_key[i][head] = mm(d_scores, query)
            part = mm_rows(k_refs[i][...], d_scores)
            grad = part if grad is None else grad + part
        d_query.append(grad[:HD] if head == 0 else grad[HD:])
    dq_ref[...] = (jnp.concatenate(d_query, 0).T * scale).astype(BF)
    for i in range(count):
        dk_refs[i][...] = (jnp.where(first, *d_key[i]) * scale).astype(BF)
        dv_refs[i][...] = jnp.where(first, *d_value[i]).astype(BF)


def attend_back(query, d_mixed, mixed, lse, keyed, mask):
    rows, model = query.shape
    count, pairs = len(keyed), model // 128
    at = lambda base: pl.BlockSpec((rows, 128), lambda j: (0, base + j))
    out = jax.ShapeDtypeStruct((rows, model), BF)
    outs = pl.pallas_call(
        functools.partial(attend_back_kernel, count, HD**-0.5),
        grid=(pairs,),
        in_specs=[at(0)] * 3
        + [pl.BlockSpec((1, 8, rows), lambda j: (j, 0, 0))]
        + [pl.BlockSpec((count, rows, 128), lambda j: (0, 0, 0))]
        + [at(0)] * count
        + [at(pairs)] * count,
        out_specs=[at(0)] * (1 + 2 * count),
        out_shape=[out] * (1 + 2 * count),
        compiler_params=pltpu.CompilerParams(vmem_limit_bytes=56 << 20),
        name="attend_back",
    )(query, d_mixed, mixed, lse, mask, *keyed, *keyed)
    return outs[0], outs[1 : 1 + count], outs[1 + count :]


def forward_layer(grid, group_bits, hidden, params, mask):
    flat_low = hidden.astype(BF)
    keyed = (mm(flat_low, params["kv"]) + params["kv_bias"]).astype(BF)
    pieces = [keyed]
    for bit in group_bits:
        pieces = pieces + [grid.flip(v, bit) for v in pieces]
    query = (mm(flat_low, params["q"]) + params["q_bias"]).astype(BF)
    mixed, lse = attend(query, pieces, mask)
    joined = hidden + mm(mixed, params["out"]) + params["out_bias"]
    first = normalize(joined, params["first_gain"], params["first_shift"])
    first_low = first.astype(BF)
    inner = mm(first_low, params["up"]) + params["up_bias"]
    act_low = activate(inner).astype(BF)
    summed = first + mm(act_low, params["down"]) + params["down_bias"]
    result = normalize(summed, params["second_gain"], params["second_shift"])
    return result, (flat_low, query, pieces, mixed, lse, joined, first_low, inner, act_low, summed)


def backward_layer(grid, group_bits, grad_out, saved, params, mask):
    flat_low, query, pieces, mixed, lse, joined, first_low, inner, act_low, summed = saved
    _, second_back = jax.vjp(normalize, summed, params["second_gain"], params["second_shift"])
    d_summed, d_second_gain, d_second_shift = second_back(grad_out)
    d_down = d_summed.astype(BF)
    d_act = mm_back(d_down, params["down"])
    _, act_back = jax.vjp(activate, inner)
    d_inner = act_back(d_act)[0].astype(BF)
    d_first = d_summed + mm_back(d_inner, params["up"])
    _, first_back = jax.vjp(normalize, joined, params["first_gain"], params["first_shift"])
    d_joined, d_first_gain, d_first_shift = first_back(d_first)
    d_branch = d_joined.astype(BF)
    d_mixed = mm_back(d_branch, params["out"]).astype(BF)
    d_query, d_keys, d_values = attend_back(query, d_mixed, mixed, lse, pieces, mask)
    for bit in reversed(group_bits):
        half = len(d_keys) // 2

        def join(values):
            return [
                (mine.astype(F32) + grid.flip(sent, bit).astype(F32)).astype(BF)
                for mine, sent in zip(values[:half], values[half:])
            ]

        d_keys, d_values = join(d_keys), join(d_values)
    d_key, d_value = d_keys[0], d_values[0]
    model = d_key.shape[1]
    d_hidden = (
        d_joined
        + mm_back(d_query, params["q"])
        + mm_back(d_key, params["kv"][:, :model])
        + mm_back(d_value, params["kv"][:, model:])
    )
    weights = {
        "down": mm_rows(act_low, d_down),
        "out_up": jnp.concatenate([mm_rows(mixed, d_branch), mm_rows(first_low, d_inner)], 1),
        "qkv": mm_rows(flat_low, jnp.concatenate([d_query, d_key, d_value], 1)),
    }
    vectors = (
        column_sum(d_query),
        column_sum(d_value),
        column_sum(d_branch),
        d_first_gain,
        d_first_shift,
        column_sum(d_down),
        d_second_gain,
        d_second_shift,
        column_sum(d_inner),
    )
    return weights, vectors, d_hidden


def local(n_dp, n_ctx, tokens, lengths, teacher, *shards):
    (
        query_weight,
        query_bias,
        key_weight,
        value_weight,
        value_bias,
        out_weight,
        out_bias,
        first_gain,
        first_shift,
        up_weight,
        up_bias,
        down_weight,
        down_bias,
        second_gain,
        second_shift,
    ) = shards
    grid = Grid(n_dp, n_ctx)
    width, seqs, model = tokens.shape
    hidden_units = up_weight.shape[1]
    rows = query_weight.shape[0]
    block = rows * n_ctx

    spread = n_ctx // (2 * seqs)
    mine = grid.ctx // spread
    member = grid.core * spread + grid.ctx % spread
    group_bits = [1 << i for i in range(spread.bit_length() - 1)] + [grid.core_bit]

    def route(turn):
        pairs = []
        for pair in range(n_dp // 2):
            for core in range(2):
                for at in range(n_ctx):
                    seq = core * seqs + (at + turn) % seqs
                    to = at // seqs
                    there = (pair * 2 + to // spread) * n_ctx + seq * spread + to % spread
                    pairs.append(((pair * 2 + core) * n_ctx + at, there))
        return pairs

    def to_groups(values):
        return jnp.concatenate(
            [
                lax.ppermute(
                    lax.dynamic_index_in_dim(values, (grid.ctx + turn) % seqs, 1, keepdims=False),
                    AXES,
                    route(turn),
                )
                for turn in range(seqs)
            ],
            0,
        )

    def from_groups(values):
        got = [
            lax.ppermute(
                values[turn * width : (turn + 1) * width],
                AXES,
                [(there, here) for here, there in route(turn)],
            )
            for turn in range(seqs)
        ]
        return jnp.stack(
            [
                functools.reduce(
                    lambda a, t: jnp.where((grid.ctx + t) % seqs == seq, got[t], a),
                    range(1, seqs),
                    got[0],
                )
                for seq in range(seqs)
            ],
            1,
        )

    vectors = (
        query_bias,
        value_bias,
        out_bias,
        first_gain,
        first_shift,
        down_bias,
        second_gain,
        second_shift,
    )
    small = jnp.concatenate(
        [jnp.stack(vectors, 1), up_bias.reshape(rows, -1), jnp.zeros((rows, 116), BF)], 1
    )
    first_part = jnp.concatenate([query_weight, key_weight, value_weight, small], 1)
    first_part = gather_ctx(grid, first_part)
    start = to_groups(tokens)
    whole_q, whole_kv, whole_small = assemble(
        grid,
        gather_top(grid, first_part),
        block,
        [
            (0, model, 0, 0, block, 0),
            (model, 2 * model, 1, 0, block, 0),
            (3 * model, 128, 2, 0, block, 0),
        ],
        [(model, model), (model, 2 * model), (model, 128)],
    )
    second_part = gather_ctx(grid, jnp.concatenate([out_weight, up_weight], 1))
    third_part = gather_ctx(grid, down_weight)
    folds = third_part.shape[0] // block
    second_part = jnp.concatenate([second_part] + jnp.split(third_part, folds, 0), 1)
    base = model + hidden_units
    whole_out, whole_up, whole_down = assemble(
        grid,
        gather_top(grid, second_part),
        block,
        [(0, model, 0, 0, block, 0), (model, hidden_units, 1, 0, block, 0)]
        + [(base + f * model, model, 2, 0, folds * block, f * block) for f in range(folds)],
        [(model, model), (model, hidden_units), (hidden_units, model)],
    )
    flat_small = whole_small[:, :12].astype(F32)
    by_vector = flat_small[:, :8].T
    params = {
        "q": whole_q,
        "kv": whole_kv,
        "out": whole_out,
        "up": whole_up,
        "down": whole_down,
        "q_bias": by_vector[0],
        "kv_bias": jnp.concatenate([jnp.zeros((model,), F32), by_vector[1]]),
        "out_bias": by_vector[2],
        "first_gain": by_vector[3],
        "first_shift": by_vector[4],
        "down_bias": by_vector[5],
        "second_gain": by_vector[6],
        "second_shift": by_vector[7],
        "up_bias": flat_small[:, 8:12].reshape(hidden_units),
    }

    both = lax.all_gather(lengths, "dp", axis=0, tiled=True)
    length = both[(grid.dp // 2) * 2 * seqs + mine]

    def slots_of(who):
        place = jnp.arange(width, dtype=jnp.int32)
        return jnp.concatenate(
            [width * (seqs * who + (mine + turn) % seqs) + place for turn in range(seqs)]
        )

    live = (slots_of(member) < length).astype(F32)[:, None]
    relative = [0]
    for bit in group_bits:
        relative = relative + [r ^ (spread if bit == grid.core_bit else bit) for r in relative]
    excluded = jnp.stack([jnp.where(slots_of(member ^ r) < length, 0.0, MASKED) for r in relative])
    mask = jnp.where(jnp.arange(128) % HD == 0, excluded[:, :, None], 0.0).astype(BF)

    middle, first_saved = forward_layer(grid, group_bits, start.astype(F32), params, mask)
    result, second_saved = forward_layer(grid, group_bits, middle, params, mask)
    layer_out = from_groups(result.astype(BF))
    diff = (result - to_groups(teacher).astype(F32)) * live
    sums = jnp.zeros((8, 128), F32).at[0, 0].set(jnp.sum(diff * diff)).at[0, 1].set(jnp.sum(live))
    for index in range(grid.n.bit_length() - 1):
        sums = sums + grid.flip(sums, 1 << index)
    loss = sums[0, 0] / (sums[0, 1] * model)

    weights_b, vectors_b, d_middle = backward_layer(
        grid, group_bits, diff, second_saved, params, mask
    )
    weights_a, vectors_a, d_start = backward_layer(
        grid, group_bits, d_middle, first_saved, params, mask
    )
    weights = jax.tree.map(jnp.add, weights_b, weights_a)
    vectors = jax.tree.map(jnp.add, vectors_b, vectors_a)
    small = jnp.concatenate(
        [jnp.stack(vectors[:8], 1), vectors[8].reshape(model, -1), jnp.zeros((model, 116), F32)], 1
    )
    grad_down = scatter_sum(grid, weights["down"])
    grad_out_up = scatter_sum(grid, weights["out_up"])
    grad_rest = scatter_sum(grid, jnp.concatenate([weights["qkv"], small], 1))
    grad_tokens = from_groups(d_start.astype(BF))
    grad_small = grad_rest[:, 3 * model :]
    vector = [grad_small[:, i] for i in range(8)]
    return (
        layer_out,
        loss,
        grad_tokens,
        grad_rest[:, :model],
        vector[0],
        grad_rest[:, model : 2 * model],
        grad_rest[:, 2 * model : 3 * model],
        vector[1],
        grad_out_up[:, :model],
        vector[2],
        vector[3],
        vector[4],
        grad_out_up[:, model:],
        grad_small[:, 8:12].reshape(-1),
        grad_down,
        vector[5],
        vector[6],
        vector[7],
    )


def solution(mesh):
    matrix, vector = P(AXES, None), P(AXES)
    states = P("ctx", "dp", None)
    params = (
        matrix,
        vector,
        matrix,
        matrix,
        vector,
        matrix,
        vector,
        vector,
        vector,
        matrix,
        vector,
        matrix,
        vector,
        vector,
        vector,
    )
    return jax.shard_map(
        functools.partial(local, mesh.shape["dp"], mesh.shape["ctx"]),
        mesh=mesh,
        in_specs=(states, P("dp"), states) + params,
        out_specs=(states, P(), states) + params,
        check_vma=False,
    )
```

```python
import functools

import jax
import jax.numpy as jnp
from jax import lax
from jax.experimental import pallas as pl
from jax.experimental.pallas import tpu as pltpu
from jax.sharding import PartitionSpec as P

H = 12
HD = 64
EPSILON = 1e-12
MASKED = -1e30
LOG2E = 1.4426950408889634
AXES = ("dp", "ctx")
BF = jnp.bfloat16
F32 = jnp.float32


def mm(left, right):
    return jnp.dot(left, right, preferred_element_type=F32)


def mm_rows(left, right):
    return lax.dot_general(left, right, (((0,), (0,)), ((), ())), preferred_element_type=F32)


def mm_back(left, right):
    return lax.dot_general(left, right, (((1,), (1,)), ((), ())), preferred_element_type=F32)


def normalize(values, gain, shift):
    centre = values - jnp.mean(values, axis=-1, keepdims=True)
    spread = jnp.mean(centre * centre, axis=-1, keepdims=True)
    return centre * lax.rsqrt(spread + EPSILON) * gain + shift


def activate(values):
    return jax.nn.gelu(values, approximate=True)


def column_sum(values):
    return jnp.sum(values.astype(F32), axis=0)


class Grid:
    def __init__(self, n_dp, n_ctx):
        self.n_dp, self.n_ctx, self.n = n_dp, n_ctx, n_dp * n_ctx
        self.dp, self.ctx = lax.axis_index("dp"), lax.axis_index("ctx")
        self.lin = self.dp * n_ctx + self.ctx
        self.ctx_bits = [1 << i for i in range(n_ctx.bit_length() - 1)]
        self.core_bit = n_ctx
        self.top_bits = [2 * n_ctx << i for i in range(n_dp.bit_length() - 2)]
        self.core = self.dp % 2

    def flip(self, value, mask):
        return lax.ppermute(value, AXES, [(i, i ^ mask) for i in range(self.n)])

    def bit(self, mask):
        return (self.lin // mask) % 2


def after(value, *others):
    return lax.optimization_barrier((value, others))[0]


def join_ctx(grid, parts, got, mask):
    got = jnp.split(got, len(parts), 0)
    low = grid.bit(mask) == 0
    return [
        jnp.where(low == first, mine, other)
        for mine, other in zip(parts, got)
        for first in (True, False)
    ]


def side_by_side(parts, axis=0):
    return jnp.concatenate(parts, axis) if len(parts) > 1 else parts[0]


class Gather:
    def __init__(self, grid, part):
        self.grid, self.part = grid, part
        self.pair = len(grid.top_bits) == 2
        self.cut = part.shape[1] // 256 * 128

    def cross(self, value):
        return self.grid.flip(value, self.grid.core_bit)

    def first(self):
        if self.pair:
            moved = [self.grid.flip(self.part, bit) for bit in self.grid.top_bits]
            return moved, self.cross(self.part)
        pieces = [(0, self.part)]
        for bit in self.grid.top_bits:
            pieces += [(m ^ bit, self.grid.flip(v, bit)) for m, v in pieces]
        self.masks = [m for m, _ in pieces]
        return [v for _, v in pieces], [self.cross(v) for _, v in pieces]

    def second(self, moved, crossed):
        if not self.pair:
            return moved, crossed
        by_a, by_b = moved
        a, b = self.grid.top_bits
        left = self.grid.flip(by_b[:, : self.cut], a)
        right = self.grid.flip(by_a[:, self.cut :], b)
        return [by_a, by_b, left, right], [crossed, self.cross(jnp.concatenate(moved, 0))]

    def finish(self, moved, crossed):
        core = self.grid.core_bit
        if self.pair:
            a, b = self.grid.top_bits
            own, both = crossed
            masks, starts = [0, a, b, a ^ b, a ^ b], [0, 0, 0, 0, self.cut]
            sides = jnp.split(both, 2, 0)
            crossed = [own, *sides, self.cross(moved[2]), self.cross(moved[3])]
            moved = [self.part, *moved]
        else:
            masks, starts = self.masks, [0] * len(moved)
        pieces = list(zip(masks, starts, moved))
        pieces += [(m ^ core, c, v) for m, c, v in zip(masks, starts, crossed)]
        return [(m // self.grid.n_ctx, c, v) for m, c, v in pieces]


def meet(*values):
    return lax.optimization_barrier(values)


def assemble(grid, pieces, rows, targets, shapes):
    copies = []
    for number, (rel, start, value) in enumerate(pieces):
        for first, columns, array, column, height, offset in targets:
            low, high = max(first, start), min(first + columns, start + value.shape[1])
            if low < high:
                copies.append((number, rel, low - start, high - low, array, column + low - first, height, offset))

    def kernel(me, *refs):
        sources, outs, sems = refs[: len(pieces)], refs[len(pieces) : -1], refs[-1]
        started = []
        for i, (number, rel, source, columns, array, column, height, offset) in enumerate(copies):
            row = pl.multiple_of((me[0] ^ rel) * height + offset, 16)
            copy = pltpu.make_async_copy(
                sources[number].at[:, pl.ds(source, columns)],
                outs[array].at[pl.ds(row, rows), pl.ds(column, columns)],
                sems.at[i],
            )
            copy.start()
            started.append(copy)
        for copy in started:
            copy.wait()

    return pl.pallas_call(
        kernel,
        out_shape=[jax.ShapeDtypeStruct(s, BF) for s in shapes],
        grid_spec=pltpu.PrefetchScalarGridSpec(
            num_scalar_prefetch=1,
            grid=(1,),
            in_specs=[pl.BlockSpec(memory_space=pl.ANY)] * len(pieces),
            out_specs=[pl.BlockSpec(memory_space=pltpu.VMEM)] * len(shapes),
            scratch_shapes=[pltpu.SemaphoreType.DMA((len(copies),))],
        ),
        name="assemble",
    )(grid.dp.reshape(1), *[v for _, _, v in pieces])


def grads_kernel(count, top, whole, core, *refs):
    lefts, rights = refs[:count], refs[count : 2 * count]
    send, keep, total = refs[-3:]
    block = total.shape[0] // (2 * (top if whole else 1))
    total[...] = sum(mm_rows(left[...], right[...]) for left, right in zip(lefts, rights))
    for i in range(top if whole else 1):
        theirs = pl.multiple_of((2 * i + 1 - core[0]) * block, 8)
        ours = pl.multiple_of((2 * i + core[0]) * block, 8)
        send[i] = total[pl.ds(theirs, block), :].astype(BF)
        keep[i] = total[pl.ds(ours, block), :]


def grads(grid, lefts, rights, columns=None, column=0, into=None):
    rows, height = lefts[0].shape
    width = rights[0].shape[1]
    columns = width if columns is None else columns
    count, top = len(lefts), grid.n_dp // 2
    block = height // (2 * top)
    whole = 2 * block % 128 != 0
    if whole:
        tile = width if width < 1536 else 768
        steps, tall, base = width // tile, height, column // tile
        left = pl.BlockSpec((rows, height), lambda i, c: (0, 0))
        right = pl.BlockSpec((rows, tile), lambda i, c: (0, i))
        out = pl.BlockSpec((top, block, tile), lambda i, c: (0, 0, base + i))
    else:
        tile, steps, tall = width, top, 2 * block
        left = pl.BlockSpec((rows, tall), lambda i, c: (0, i))
        right = pl.BlockSpec((rows, width), lambda i, c: (0, 0))
        out = pl.BlockSpec((1, block, width), lambda i, c: (i, 0, 0))
    earlier = [] if into is None else list(into)
    return pl.pallas_call(
        functools.partial(grads_kernel, count, top, whole),
        out_shape=[
            jax.ShapeDtypeStruct((top, block, columns), BF),
            jax.ShapeDtypeStruct((top, block, columns), F32),
        ],
        grid_spec=pltpu.PrefetchScalarGridSpec(
            num_scalar_prefetch=1,
            grid=(steps,),
            in_specs=[left] * count
            + [right] * count
            + [pl.BlockSpec(memory_space=pl.ANY)] * len(earlier),
            out_specs=[out] * 2,
            scratch_shapes=[pltpu.VMEM((tall, tile), F32)],
        ),
        input_output_aliases={1 + 2 * count + i: i for i in range(len(earlier))},
        compiler_params=pltpu.CompilerParams(vmem_limit_bytes=56 << 20),
        name="grads",
    )(grid.core.reshape(1), *lefts, *rights, *earlier)


class Reduce:
    def __init__(self, grid):
        self.grid, self.sends, self.parts = grid, [], []

    def add(self, send, keep):
        self.parts.append((keep, self.grid.flip(send, self.grid.core_bit)))

    def step(self, value, mask, axis):
        bit = self.grid.bit(mask)
        pick = functools.partial(lax.dynamic_index_in_dim, axis=axis, keepdims=False)
        send = pick(value, 1 - bit).astype(BF)
        self.sends = self.sends + [send]
        return pick(value, bit), self.grid.flip(send, mask)

    def sent(self):
        sends, self.sends = self.sends, []
        return sends

    def first(self, *others):
        got = after([g for _, g in self.parts], *others)
        value = side_by_side([k + g.astype(F32) for (k, _), g in zip(self.parts, got)], -1)
        top, self.block, self.width = value.shape
        if len(self.grid.top_bits) == 2:
            a, b = self.grid.top_bits
            cut = self.width // 256 * 128
            value = value.reshape(2, 2, self.block, self.width)
            self.halves = [self.step(value[..., :cut], a, 1), self.step(value[..., cut:], b, 0)]
        else:
            for mask in reversed(self.grid.top_bits):
                value = value.reshape(2, value.shape[0] // 2, self.block, self.width)
                keep, got = self.step(value, mask, 0)
                value = keep + got.astype(F32)
            self.halves = [(value[0], None)]

    def second(self, *others):
        if len(self.halves) == 2:
            a, b = self.grid.top_bits
            (left, by_a), (right, by_b) = self.halves
            by_a, by_b = after((by_a, by_b), *others)
            self.halves = [
                self.step(left + by_a.astype(F32), b, 0),
                self.step(right + by_b.astype(F32), a, 0),
            ]

    def third(self, *others):
        values = [k if g is None else k + after(g, *others).astype(F32) for k, g in self.halves]
        self.value = side_by_side(values, -1)
        self.left = list(self.grid.ctx_bits)
        self.turn()

    def turn(self):
        own = self.block // self.grid.n_ctx
        self.last = self.step(self.value.reshape(-1, 2, own, self.width), self.left.pop(0), 1)

    def fourth(self, *others):
        keep, got = self.last
        self.last = None
        self.value = (keep + after(got, *others).astype(F32)).reshape(-1, self.width)
        if self.left:
            self.turn()

    def finish_value(self):
        while self.last is not None:
            self.fourth()
        return self.value


def lanes(shape):
    return lax.broadcasted_iota(jnp.int32, shape, len(shape) - 1)


def attend_kernel(count, scale, q_ref, mask_ref, *refs):
    k_refs, v_refs = refs[:count], refs[count : 2 * count]
    o_ref, lse_ref = refs[2 * count :]
    rows = q_ref.shape[0]
    factor = scale * LOG2E
    lane = lanes((rows, 128))
    first = lane < HD
    one = jnp.where(lane % HD == 0, 1.0, 0.0).astype(BF)
    outs = []
    for head in range(2):
        keep = first if head == 0 else jnp.logical_not(first)
        query = jnp.where(keep, q_ref[...], one)
        scores = [
            mm_back(jnp.where(keep, k_refs[i][...], mask_ref[i]), query) for i in range(count)
        ]
        top = functools.reduce(jnp.maximum, [jnp.max(s, axis=0, keepdims=True) for s in scores])
        top = top * factor
        mixed = None
        for i in range(count):
            probs = jnp.exp2(scores[i] * factor - top).astype(BF)
            value = jnp.where(keep, v_refs[i][...], jnp.ones((), BF))
            part = mm_rows(value, probs)
            mixed = part if mixed is None else mixed + part
        if head == 0:
            total, mixed = mixed[HD : HD + 1], mixed[:HD]
        else:
            total, mixed = mixed[:1], mixed[HD:]
        outs.append(mixed / total)
        lse_ref[0, head : head + 1, :] = top + jnp.log2(total)
    o_ref[...] = jnp.concatenate(outs, 0).T.astype(BF)


def attend(query, keyed, mask, begin=0, pairs=None, into=None):
    rows, model = query.shape
    count, every = len(keyed), model // 128
    pairs = every if pairs is None else pairs
    at = lambda base: pl.BlockSpec((rows, 128), lambda j: (0, base + begin + j))
    earlier = [] if into is None else list(into)

    def kernel(*refs):
        inputs = 2 + 2 * count
        attend_kernel(count, HD**-0.5, *refs[:inputs], *refs[inputs + len(earlier) :])

    return pl.pallas_call(
        kernel,
        grid=(pairs,),
        in_specs=[at(0), pl.BlockSpec((count, rows, 128), lambda j: (0, 0, 0))]
        + [at(0)] * count
        + [at(every)] * count
        + [pl.BlockSpec(memory_space=pl.ANY)] * len(earlier),
        out_specs=[at(0), pl.BlockSpec((1, 8, rows), lambda j: (begin + j, 0, 0))],
        out_shape=[
            jax.ShapeDtypeStruct((rows, model), BF),
            jax.ShapeDtypeStruct((every, 8, rows), F32),
        ],
        input_output_aliases={2 + 2 * count + i: i for i in range(len(earlier))},
        compiler_params=pltpu.CompilerParams(vmem_limit_bytes=56 << 20),
        name="attend",
    )(query, mask, *keyed, *keyed, *earlier)


def attend_back_kernel(count, scale, q_ref, do_ref, o_ref, lse_ref, mask_ref, *refs):
    k_refs, v_refs = refs[:count], refs[count : 2 * count]
    dq_ref = refs[2 * count]
    dkv_refs = refs[2 * count + 1 :]
    rows = q_ref.shape[0]
    factor = scale * LOG2E
    lane = lanes((rows, 128))
    first = lane < HD
    one = jnp.where(lane % HD == 0, 1.0, 0.0).astype(BF)
    two = jnp.where(lane % HD < 2, 1.0, 0.0).astype(BF)
    wide = do_ref[...].astype(F32)
    product = wide * o_ref[...].astype(F32)
    d_query = []
    keeps = (first, jnp.logical_not(first))
    d_key = [[None] * 2 for _ in range(count)]
    d_value = [[None] * 2 for _ in range(count)]
    for head in range(2):
        keep = keeps[head]
        query = jnp.where(keep, q_ref[...], one)
        delta = jnp.sum(jnp.where(keep, product, 0.0), axis=1, keepdims=True)
        high = delta.astype(BF).astype(F32)
        spare = lane % HD
        extra = jnp.where(spare == 0, -high, jnp.where(spare == 1, high - delta, 0.0))
        d_out = jnp.where(keep, wide, extra).astype(BF)
        lse = lse_ref[0, head : head + 1, :]
        grad = None
        for i in range(count):
            key = jnp.where(keep, k_refs[i][...], mask_ref[i])
            scores = mm_back(key, query)
            probs = jnp.exp2(scores * factor - lse)
            d_probs = mm_back(jnp.where(keep, v_refs[i][...], two), d_out)
            d_scores = (probs * d_probs).astype(BF)
            d_value[i][head] = mm(probs.astype(BF), do_ref[...])
            d_key[i][head] = mm(d_scores, query)
            part = mm_rows(k_refs[i][...], d_scores)
            grad = part if grad is None else grad + part
        d_query.append(grad[:HD] if head == 0 else grad[HD:])
    dq_ref[...] = (jnp.concatenate(d_query, 0).T * scale).astype(BF)
    for i in range(count):
        dkv_refs[i][0] = (jnp.where(first, *d_key[i]) * scale).astype(BF)
        dkv_refs[i][1] = jnp.where(first, *d_value[i]).astype(BF)


def attend_back(query, d_mixed, mixed, lse, keyed, mask, begin, pairs):
    rows, model = query.shape
    count, every = len(keyed), model // 128
    at = lambda base: pl.BlockSpec((rows, 128), lambda j: (0, base + begin + j))
    outs = pl.pallas_call(
        functools.partial(attend_back_kernel, count, HD**-0.5),
        grid=(pairs,),
        in_specs=[at(0)] * 3
        + [pl.BlockSpec((1, 8, rows), lambda j: (begin + j, 0, 0))]
        + [pl.BlockSpec((count, rows, 128), lambda j: (0, 0, 0))]
        + [at(0)] * count
        + [at(every)] * count,
        out_specs=[pl.BlockSpec((rows, 128), lambda j: (0, j))]
        + [pl.BlockSpec((2, rows, 128), lambda j: (0, 0, j))] * count,
        out_shape=[jax.ShapeDtypeStruct((rows, pairs * 128), BF)]
        + [jax.ShapeDtypeStruct((2, rows, pairs * 128), BF)] * count,
        compiler_params=pltpu.CompilerParams(vmem_limit_bytes=56 << 20),
        name="attend_back",
    )(query, d_mixed, mixed, lse, mask, *keyed, *keyed)
    return outs[0], list(outs[1:])


def forward_layer(grid, group_bits, hidden, params, mask, hooks=None):
    flat_low = hidden.astype(BF)
    keyed = (mm(flat_low, params["kv"]) + params["kv_bias"]).astype(BF)
    pieces = [keyed]
    for bit in group_bits:
        pieces = pieces + [grid.flip(v, bit) for v in pieces]
    query = (mm(flat_low, params["q"]) + params["q_bias"]).astype(BF)
    if hooks is None:
        mixed, lse = attend(query, pieces, mask)
    else:
        pairs = query.shape[1] // 128
        part = attend(query, pieces, mask, 0, pairs // 2)
        query, part, waiting = hooks[0](query, part)
        mixed, lse = attend(query, pieces, mask, pairs // 2, pairs - pairs // 2, part)
        mixed, more, waiting = hooks[1](mixed, waiting)
        params.update(more)
    joined = hidden + mm(mixed, params["out"]) + params["out_bias"]
    first = normalize(joined, params["first_gain"], params["first_shift"])
    first_low = first.astype(BF)
    if hooks is not None:
        first_low, waiting = hooks[2](first_low, waiting)
    inner = mm(first_low, params["up"]) + params["up_bias"]
    act_low = activate(inner).astype(BF)
    if hooks is not None:
        act_low, more = hooks[3](act_low, waiting)
        params.update(more)
    summed = first + mm(act_low, params["down"]) + params["down_bias"]
    result = normalize(summed, params["second_gain"], params["second_shift"])
    return result, (flat_low, query, pieces, mixed, lse, joined, first_low, inner, act_low, summed)


class Backward:
    def __init__(self, grid, group_bits, saved, params, mask):
        self.grid, self.group_bits, self.params, self.mask = grid, group_bits, params, mask
        (
            self.flat_low,
            self.query,
            self.pieces,
            self.mixed,
            self.lse,
            self.joined,
            self.first_low,
            self.inner,
            self.act_low,
            self.summed,
        ) = saved

    def top(self, grad_out):
        p = self.params
        _, back = jax.vjp(normalize, self.summed, p["second_gain"], p["second_shift"])
        self.d_summed, self.d_second_gain, self.d_second_shift = back(grad_out)
        self.d_down = self.d_summed.astype(BF)

    def hidden_units(self):
        d_act = mm_back(self.d_down, self.params["down"])
        _, act_back = jax.vjp(activate, self.inner)
        self.d_inner = act_back(d_act)[0].astype(BF)

    def middle(self):
        p = self.params
        d_first = self.d_summed + mm_back(self.d_inner, p["up"])
        _, back = jax.vjp(normalize, self.joined, p["first_gain"], p["first_shift"])
        self.d_joined, self.d_first_gain, self.d_first_shift = back(d_first)
        self.d_branch = self.d_joined.astype(BF)

    def attention(self, begin, pairs):
        d_query, d_keyed = attend_back(
            self.query, self.d_mixed, self.mixed, self.lse, self.pieces, self.mask, begin, pairs
        )
        for bit in reversed(self.group_bits):
            half = len(d_keyed) // 2
            sent = [self.grid.flip(v, bit) for v in d_keyed[half:]]
            d_keyed = [
                (mine.astype(F32) + got.astype(F32)).astype(BF)
                for mine, got in zip(d_keyed[:half], sent)
            ]
        return d_query, d_keyed[0]

    def collect(self, parts):
        self.d_query = side_by_side([q for q, _ in parts], 1)
        self.d_keyed = jnp.concatenate([kv[i] for i in range(2) for _, kv in parts], 1)

    def start(self):
        return (
            self.d_joined
            + mm_back(self.d_query, self.params["q"])
            + mm_back(self.d_keyed, self.params["kv"])
        )

    def vectors(self):
        model = self.d_query.shape[1]
        rows = (
            column_sum(self.d_query),
            column_sum(self.d_keyed[:, model:]),
            column_sum(self.d_branch),
            self.d_first_gain,
            self.d_first_shift,
            column_sum(self.d_down),
            self.d_second_gain,
            self.d_second_shift,
        )
        return rows, column_sum(self.d_inner)


def local(n_dp, n_ctx, tokens, lengths, teacher, *shards):
    (
        query_weight,
        query_bias,
        key_weight,
        value_weight,
        value_bias,
        out_weight,
        out_bias,
        first_gain,
        first_shift,
        up_weight,
        up_bias,
        down_weight,
        down_bias,
        second_gain,
        second_shift,
    ) = shards
    grid = Grid(n_dp, n_ctx)
    width, seqs, model = tokens.shape
    inner_width = up_weight.shape[1]
    rows = query_weight.shape[0]
    block = rows * n_ctx

    spread = n_ctx // (2 * seqs)
    mine = grid.ctx // spread
    member = grid.core * spread + grid.ctx % spread
    group_bits = [1 << i for i in range(spread.bit_length() - 1)] + [grid.core_bit]

    def route(turn):
        pairs = []
        for pair in range(n_dp // 2):
            for core in range(2):
                for at in range(n_ctx):
                    seq = core * seqs + (at + turn) % seqs
                    to = at // seqs
                    there = (pair * 2 + to // spread) * n_ctx + seq * spread + to % spread
                    pairs.append(((pair * 2 + core) * n_ctx + at, there))
        return pairs

    def to_group(values, turn):
        value = lax.dynamic_index_in_dim(values, (grid.ctx + turn) % seqs, 1, keepdims=False)
        return lax.ppermute(value, AXES, route(turn))

    def to_groups(values):
        return jnp.concatenate([to_group(values, turn) for turn in range(seqs)], 0)

    def from_groups(values):
        got = [
            lax.ppermute(
                values[turn * width : (turn + 1) * width],
                AXES,
                [(there, here) for here, there in route(turn)],
            )
            for turn in range(seqs)
        ]
        return jnp.stack(
            [
                functools.reduce(
                    lambda a, t: jnp.where((grid.ctx + t) % seqs == seq, got[t], a),
                    range(1, seqs),
                    got[0],
                )
                for seq in range(seqs)
            ],
            1,
        )

    turns = list(reversed(grid.ctx_bits))
    vectors = (
        query_bias,
        value_bias,
        out_bias,
        first_gain,
        first_shift,
        down_bias,
        second_gain,
        second_shift,
    )
    one = [jnp.concatenate([query_weight, key_weight, value_weight], 1)]
    small = [
        jnp.concatenate(
            [jnp.stack(vectors, 0).T, up_bias.reshape(rows, -1), jnp.zeros((rows, 116), BF)], 1
        )
    ]
    two, three = [jnp.concatenate([out_weight, up_weight], 1)], [down_weight]
    last = len(turns) - 1
    got_two = None
    for i, turn in enumerate(turns):
        got = [grid.flip(side_by_side(v), turn) for v in (one, small)]
        if got_two is not None:
            two = join_ctx(grid, two, got_two, turns[i - 2])
        got_two = grid.flip(side_by_side(two), turns[i - 1]) if i else None
        got, got_two, two, tokens = meet(got, got_two, two, tokens)
        one, small = join_ctx(grid, one, got[0], turn), join_ctx(grid, small, got[1], turn)
    if got_two is not None:
        two = join_ctx(grid, two, got_two, turns[last - 1])
    first = Gather(grid, jnp.concatenate([side_by_side(one), side_by_side(small)], 1))
    got, start, two, tokens = meet(
        first.first(), [to_group(tokens, turn) for turn in range(seqs - 1)], two, tokens
    )
    more, crossed = first.second(*got)
    got_two = grid.flip(side_by_side(two), turns[last])
    more, crossed, start, got_two, two, three = meet(
        more, crossed, start + [to_group(tokens, seqs - 1)], got_two, two, three
    )
    second = Gather(grid, side_by_side(join_ctx(grid, two, got_two, turns[last])))
    second_got = second.first()
    for turn in turns[:-1]:
        three = join_ctx(grid, three, grid.flip(side_by_side(three), turn), turn)
    start = jnp.concatenate(start, 0)
    whole_q, whole_kv, whole_small = assemble(
        grid,
        first.finish(more, crossed),
        block,
        [
            (0, model, 0, 0, block, 0),
            (model, 2 * model, 1, 0, block, 0),
            (3 * model, 128, 2, 0, block, 0),
        ],
        [(model, model), (model, 2 * model), (model, 128)],
    )
    flat_small = whole_small[:, :12].astype(F32)
    by_vector = flat_small[:, :8].T
    params = {
        "q": whole_q,
        "kv": whole_kv,
        "q_bias": by_vector[0],
        "kv_bias": jnp.concatenate([jnp.zeros((model,), F32), by_vector[1]]),
        "out_bias": by_vector[2],
        "first_gain": by_vector[3],
        "first_shift": by_vector[4],
        "down_bias": by_vector[5],
        "second_gain": by_vector[6],
        "second_shift": by_vector[7],
        "up_bias": flat_small[:, 8:12].reshape(inner_width),
    }

    theirs = grid.flip(lengths, grid.core_bit)
    length = jnp.where(mine // seqs == grid.core, lengths[mine % seqs], theirs[mine % seqs])

    def slots_of(who):
        place = jnp.arange(width, dtype=jnp.int32)
        return jnp.concatenate(
            [width * (seqs * who + (mine + turn) % seqs) + place for turn in range(seqs)]
        )

    live = (slots_of(member) < length).astype(F32)[:, None]
    relative = [0]
    for bit in group_bits:
        relative = relative + [r ^ (spread if bit == grid.core_bit else bit) for r in relative]
    excluded = jnp.stack([jnp.where(slots_of(member ^ r) < length, 0.0, MASKED) for r in relative])
    mask = jnp.where(jnp.arange(128) % HD == 0, excluded[:, :, None], 0.0).astype(BF)

    def middle_of_attention(query, part):
        query, part, got, parts = meet(query, part, second_got, three)
        state = second.second(*got)
        return query, part, (state, parts, grid.flip(side_by_side(parts), turns[last]))

    def after_attention(mixed, waiting):
        mixed, (more, crossed), parts, got = meet(mixed, *waiting)
        third = Gather(grid, side_by_side(join_ctx(grid, parts, got, turns[last])))
        got = third.first()
        whole_out, whole_up = assemble(
            grid,
            second.finish(more, crossed),
            block,
            [(0, model, 0, 0, block, 0), (model, inner_width, 1, 0, block, 0)],
            [(model, model), (model, inner_width)],
        )
        return mixed, {"out": whole_out, "up": whole_up}, (third, got)

    def before_up(first_low, waiting):
        third, got = waiting
        first_low, got = meet(first_low, got)
        return first_low, (third, third.second(*got))

    def after_up(act_low, waiting):
        third, state = waiting
        act_low, (more, crossed) = meet(act_low, state)
        tall = third.part.shape[0]
        (whole_down,) = assemble(
            grid,
            third.finish(more, crossed),
            tall,
            [(0, model, 0, 0, tall, 0)],
            [(inner_width, model)],
        )
        return act_low, {"down": whole_down}

    hooks = (middle_of_attention, after_attention, before_up, after_up)
    middle, first_saved = forward_layer(
        grid, group_bits, start.astype(F32), params, mask, hooks
    )
    target = to_groups(after(teacher, middle))
    result, second_saved = forward_layer(grid, group_bits, middle, params, mask)
    layer_out = from_groups(result.astype(BF))
    diff = (result - target.astype(F32)) * live
    error = jnp.sum(diff * diff)

    pairs = model // 128
    b = Backward(grid, group_bits, second_saved, params, mask)
    b.top(diff)
    b.hidden_units()
    b.middle()
    b.d_mixed = mm_back(b.d_branch, params["out"]).astype(BF)
    b.collect([b.attention(0, pairs)])
    d_middle = b.start()

    a = Backward(grid, group_bits, first_saved, params, mask)
    a.top(d_middle)
    downs = grads(grid, [b.act_low, a.act_low], [b.d_down, a.d_down])
    reduce_down, reduce_up, reduce_rest = Reduce(grid), Reduce(grid), Reduce(grid)
    reduce_down.add(*downs)
    a.d_down = after(a.d_down, downs)
    a.hidden_units()
    ups = grads(grid, [b.first_low, a.first_low], [b.d_inner, a.d_inner])
    reduce_up.add(*ups)
    reduce_down.first(ups)
    a.d_inner = after(a.d_inner, ups)
    a.middle()
    outs = grads(grid, [b.mixed, a.mixed], [b.d_branch, a.d_branch])
    reduce_up.add(*outs)
    a.d_mixed = mm_back(after(a.d_branch, outs, reduce_down.sent()), params["out"]).astype(BF)
    part_one = a.attention(0, pairs // 2)
    reduce_down.second(part_one[0])
    reduce_up.first(part_one[0])
    a.d_mixed = after(a.d_mixed, part_one, reduce_down.sent(), reduce_up.sent())
    reduce_down.third(reduce_up.halves)
    part_two = a.attention(pairs // 2, pairs - pairs // 2)
    a.collect([part_one, part_two])
    lefts = [b.flat_low, a.flat_low]
    rest_q = grads(grid, lefts, [b.d_query, a.d_query])
    reduce_rest.add(*rest_q)
    reduce_up.second(rest_q)
    rest_kv = grads(grid, lefts, [b.d_keyed, a.d_keyed])
    reduce_rest.add(*rest_kv)
    reduce_down.fourth(rest_kv)
    rows_b, wide_b = b.vectors()
    rows_a, wide_a = a.vectors()
    stacked = (jnp.concatenate(rows_b) + jnp.concatenate(rows_a)).reshape(8, model)
    number = jnp.sum(live)
    whole = [(v, v.astype(BF).astype(F32)) for v in (error, number)]
    here = (jnp.arange(grid.n) == grid.lin)[None, :]
    marks = [jnp.where(here, v, 0.0) for full, low in whole for v in (low, full - low)]
    spare = -(12 + 4 * grid.n) % 128
    marks = jnp.concatenate(marks + [jnp.zeros((1, spare), F32)], 1)
    small = jnp.concatenate(
        [
            stacked.T,
            (wide_b + wide_a).reshape(model, -1),
            jnp.broadcast_to(marks, (model, marks.shape[1])),
        ],
        1,
    ).reshape(n_dp // 2, 2, block, -1)
    pick = functools.partial(lax.dynamic_index_in_dim, axis=1, keepdims=False)
    reduce_rest.add(pick(small, 1 - grid.core).astype(BF), pick(small, grid.core))
    a.d_query = after(a.d_query, rest_kv)
    d_start = a.start()
    grad_tokens = from_groups(d_start.astype(BF))
    reduce_rest.first(d_start)
    reduce_up.third(reduce_rest.sent())
    reduce_rest.second()
    reduce_up.fourth(reduce_rest.sent())
    reduce_rest.third()
    grad_down = reduce_down.finish_value()
    grad_out_up = reduce_up.finish_value()
    grad_rest = reduce_rest.finish_value()
    grad_small = grad_rest[:, 3 * model :]
    sums = jnp.sum(grad_small[:1, 12 : 12 + 4 * grid.n].reshape(4, grid.n), axis=1)
    loss = (sums[0] + sums[1]) / ((sums[2] + sums[3]) * model)
    vector = [grad_small[:, i] for i in range(8)]
    return (
        layer_out,
        loss,
        grad_tokens,
        grad_rest[:, :model],
        vector[0],
        grad_rest[:, model : 2 * model],
        grad_rest[:, 2 * model : 3 * model],
        vector[1],
        grad_out_up[:, inner_width:],
        vector[2],
        vector[3],
        vector[4],
        grad_out_up[:, :inner_width],
        grad_small[:, 8:12].reshape(-1),
        grad_down,
        vector[5],
        vector[6],
        vector[7],
    )


def solution(mesh):
    matrix, vector = P(AXES, None), P(AXES)
    states = P("ctx", "dp", None)
    params = (
        matrix,
        vector,
        matrix,
        matrix,
        vector,
        matrix,
        vector,
        vector,
        vector,
        matrix,
        vector,
        matrix,
        vector,
        vector,
        vector,
    )
    return jax.shard_map(
        functools.partial(local, mesh.shape["dp"], mesh.shape["ctx"]),
        mesh=mesh,
        in_specs=(states, P("dp"), states) + params,
        out_specs=(states, P(), states) + params,
        check_vma=False,
    )
```

```python
import functools

import jax
import jax.numpy as jnp
from jax import lax
from jax.experimental import pallas as pl
from jax.experimental.pallas import tpu as pltpu
from jax.sharding import PartitionSpec as P

H = 12
HD = 64
EPSILON = 1e-12
MASKED = -1e30
LOG2E = 1.4426950408889634
AXES = ("dp", "ctx")
BF = jnp.bfloat16
F32 = jnp.float32


def mm(left, right):
    return jnp.dot(left, right, preferred_element_type=F32)


def mm_rows(left, right):
    return lax.dot_general(left, right, (((0,), (0,)), ((), ())), preferred_element_type=F32)


def mm_back(left, right):
    return lax.dot_general(left, right, (((1,), (1,)), ((), ())), preferred_element_type=F32)


def normalize(values, gain, shift):
    centre = values - jnp.mean(values, axis=-1, keepdims=True)
    spread = jnp.mean(centre * centre, axis=-1, keepdims=True)
    return centre * lax.rsqrt(spread + EPSILON) * gain + shift


def activate(values):
    return jax.nn.gelu(values, approximate=True)


def column_sum(values):
    return jnp.sum(values.astype(F32), axis=0)


class Grid:
    def __init__(self, n_dp, n_ctx):
        self.n_dp, self.n_ctx, self.n = n_dp, n_ctx, n_dp * n_ctx
        self.dp, self.ctx = lax.axis_index("dp"), lax.axis_index("ctx")
        self.lin = self.dp * n_ctx + self.ctx
        self.ctx_bits = [1 << i for i in range(n_ctx.bit_length() - 1)]
        self.core_bit = n_ctx
        self.top_bits = [2 * n_ctx << i for i in range(n_dp.bit_length() - 2)]
        self.core = self.dp % 2

    def flip(self, value, mask):
        return lax.ppermute(value, AXES, [(i, i ^ mask) for i in range(self.n)])

    def bit(self, mask):
        return (self.lin // mask) % 2


def after(value, *others):
    return lax.optimization_barrier((value, others))[0]


def join_ctx(grid, parts, got, mask):
    got = jnp.split(got, len(parts), 0)
    low = grid.bit(mask) == 0
    return [
        jnp.where(low == first, mine, other)
        for mine, other in zip(parts, got)
        for first in (True, False)
    ]


def side_by_side(parts, axis=0):
    return jnp.concatenate(parts, axis) if len(parts) > 1 else parts[0]


class Gather:
    def __init__(self, grid, part):
        self.grid, self.part = grid, part
        self.pair = len(grid.top_bits) == 2
        self.cut = part.shape[1] // 256 * 128

    def cross(self, value):
        return self.grid.flip(value, self.grid.core_bit)

    def first(self):
        if self.pair:
            moved = [self.grid.flip(self.part, bit) for bit in self.grid.top_bits]
            return moved, self.cross(self.part)
        pieces = [(0, self.part)]
        for bit in self.grid.top_bits:
            pieces += [(m ^ bit, self.grid.flip(v, bit)) for m, v in pieces]
        self.masks = [m for m, _ in pieces]
        return [v for _, v in pieces], [self.cross(v) for _, v in pieces]

    def second(self, moved, crossed):
        if not self.pair:
            return moved, crossed
        by_a, by_b = moved
        a, b = self.grid.top_bits
        left = self.grid.flip(by_b[:, : self.cut], a)
        right = self.grid.flip(by_a[:, self.cut :], b)
        return [by_a, by_b, left, right], [crossed, self.cross(jnp.concatenate(moved, 0))]

    def finish(self, moved, crossed):
        core = self.grid.core_bit
        if self.pair:
            a, b = self.grid.top_bits
            own, both = crossed
            masks, starts = [0, a, b, a ^ b, a ^ b], [0, 0, 0, 0, self.cut]
            sides = jnp.split(both, 2, 0)
            crossed = [own, *sides, self.cross(moved[2]), self.cross(moved[3])]
            moved = [self.part, *moved]
        else:
            masks, starts = self.masks, [0] * len(moved)
        pieces = list(zip(masks, starts, moved))
        pieces += [(m ^ core, c, v) for m, c, v in zip(masks, starts, crossed)]
        return [(m // self.grid.n_ctx, c, v) for m, c, v in pieces]


def meet(*values):
    return lax.optimization_barrier(values)


def assemble(grid, pieces, rows, targets, shapes):
    copies = []
    for number, (rel, start, value) in enumerate(pieces):
        for first, columns, array, column, height, offset in targets:
            low, high = max(first, start), min(first + columns, start + value.shape[1])
            if low < high:
                copies.append((number, rel, low - start, high - low, array, column + low - first, height, offset))

    def kernel(me, *refs):
        sources, outs, sems = refs[: len(pieces)], refs[len(pieces) : -1], refs[-1]
        started = []
        for i, (number, rel, source, columns, array, column, height, offset) in enumerate(copies):
            row = pl.multiple_of((me[0] ^ rel) * height + offset, 16)
            copy = pltpu.make_async_copy(
                sources[number].at[:, pl.ds(source, columns)],
                outs[array].at[pl.ds(row, rows), pl.ds(column, columns)],
                sems.at[i],
            )
            copy.start()
            started.append(copy)
        for copy in started:
            copy.wait()

    return pl.pallas_call(
        kernel,
        out_shape=[jax.ShapeDtypeStruct(s, BF) for s in shapes],
        grid_spec=pltpu.PrefetchScalarGridSpec(
            num_scalar_prefetch=1,
            grid=(1,),
            in_specs=[pl.BlockSpec(memory_space=pl.ANY)] * len(pieces),
            out_specs=[pl.BlockSpec(memory_space=pltpu.VMEM)] * len(shapes),
            scratch_shapes=[pltpu.SemaphoreType.DMA((len(copies),))],
        ),
        name="assemble",
    )(grid.dp.reshape(1), *[v for _, _, v in pieces])


def grads_kernel(count, top, whole, core, *refs):
    lefts, rights = refs[:count], refs[count : 2 * count]
    send, keep, total = refs[-3:]
    block = total.shape[0] // (2 * (top if whole else 1))
    total[...] = sum(mm_rows(left[...], right[...]) for left, right in zip(lefts, rights))
    for i in range(top if whole else 1):
        theirs = pl.multiple_of((2 * i + 1 - core[0]) * block, 8)
        ours = pl.multiple_of((2 * i + core[0]) * block, 8)
        send[i] = total[pl.ds(theirs, block), :].astype(BF)
        keep[i] = total[pl.ds(ours, block), :]


def grads(grid, lefts, rights, columns=None, column=0, into=None):
    rows, height = lefts[0].shape
    width = rights[0].shape[1]
    columns = width if columns is None else columns
    count, top = len(lefts), grid.n_dp // 2
    block = height // (2 * top)
    whole = 2 * block % 128 != 0
    if whole:
        tile = width if width < 1536 else 768
        steps, tall, base = width // tile, height, column // tile
        left = pl.BlockSpec((rows, height), lambda i, c: (0, 0))
        right = pl.BlockSpec((rows, tile), lambda i, c: (0, i))
        out = pl.BlockSpec((top, block, tile), lambda i, c: (0, 0, base + i))
    else:
        tile, steps, tall = width, top, 2 * block
        left = pl.BlockSpec((rows, tall), lambda i, c: (0, i))
        right = pl.BlockSpec((rows, width), lambda i, c: (0, 0))
        out = pl.BlockSpec((1, block, width), lambda i, c: (i, 0, 0))
    earlier = [] if into is None else list(into)
    return pl.pallas_call(
        functools.partial(grads_kernel, count, top, whole),
        out_shape=[
            jax.ShapeDtypeStruct((top, block, columns), BF),
            jax.ShapeDtypeStruct((top, block, columns), F32),
        ],
        grid_spec=pltpu.PrefetchScalarGridSpec(
            num_scalar_prefetch=1,
            grid=(steps,),
            in_specs=[left] * count
            + [right] * count
            + [pl.BlockSpec(memory_space=pl.ANY)] * len(earlier),
            out_specs=[out] * 2,
            scratch_shapes=[pltpu.VMEM((tall, tile), F32)],
        ),
        input_output_aliases={1 + 2 * count + i: i for i in range(len(earlier))},
        compiler_params=pltpu.CompilerParams(vmem_limit_bytes=56 << 20),
        name="grads",
    )(grid.core.reshape(1), *lefts, *rights, *earlier)


class Reduce:
    def __init__(self, grid):
        self.grid, self.sends, self.parts = grid, [], []

    def add(self, send, keep):
        self.parts.append((keep, self.grid.flip(send, self.grid.core_bit)))

    def step(self, value, mask, axis):
        bit = self.grid.bit(mask)
        pick = functools.partial(lax.dynamic_index_in_dim, axis=axis, keepdims=False)
        send = pick(value, 1 - bit).astype(BF)
        self.sends = self.sends + [send]
        return pick(value, bit), self.grid.flip(send, mask)

    def sent(self):
        sends, self.sends = self.sends, []
        return sends

    def first(self, *others):
        got = after([g for _, g in self.parts], *others)
        value = side_by_side([k + g.astype(F32) for (k, _), g in zip(self.parts, got)], -1)
        top, self.block, self.width = value.shape
        if len(self.grid.top_bits) == 2:
            a, b = self.grid.top_bits
            cut = self.width // 256 * 128
            value = value.reshape(2, 2, self.block, self.width)
            self.halves = [self.step(value[..., :cut], a, 1), self.step(value[..., cut:], b, 0)]
        else:
            for mask in reversed(self.grid.top_bits):
                value = value.reshape(2, value.shape[0] // 2, self.block, self.width)
                keep, got = self.step(value, mask, 0)
                value = keep + got.astype(F32)
            self.halves = [(value[0], None)]

    def second(self, *others):
        if len(self.halves) == 2:
            a, b = self.grid.top_bits
            (left, by_a), (right, by_b) = self.halves
            by_a, by_b = after((by_a, by_b), *others)
            self.halves = [
                self.step(left + by_a.astype(F32), b, 0),
                self.step(right + by_b.astype(F32), a, 0),
            ]

    def third(self, *others):
        values = [k if g is None else k + after(g, *others).astype(F32) for k, g in self.halves]
        self.value = side_by_side(values, -1)
        self.left = list(self.grid.ctx_bits)
        self.turn()

    def turn(self):
        own = self.block // self.grid.n_ctx
        self.last = self.step(self.value.reshape(-1, 2, own, self.width), self.left.pop(0), 1)

    def fourth(self, *others):
        keep, got = self.last
        self.last = None
        self.value = (keep + after(got, *others).astype(F32)).reshape(-1, self.width)
        if self.left:
            self.turn()

    def finish_value(self):
        while self.last is not None:
            self.fourth()
        return self.value


def lanes(shape):
    return lax.broadcasted_iota(jnp.int32, shape, len(shape) - 1)


def attend_kernel(count, scale, q_ref, mask_ref, *refs):
    k_refs, v_refs = refs[:count], refs[count : 2 * count]
    o_ref, lse_ref = refs[2 * count :]
    rows = q_ref.shape[0]
    factor = scale * LOG2E
    lane = lanes((rows, 128))
    first = lane < HD
    one = jnp.where(lane % HD == 0, 1.0, 0.0).astype(BF)
    outs = []
    for head in range(2):
        keep = first if head == 0 else jnp.logical_not(first)
        query = jnp.where(keep, q_ref[...], one)
        scores = [
            mm_back(jnp.where(keep, k_refs[i][...], mask_ref[i]), query) for i in range(count)
        ]
        top = functools.reduce(jnp.maximum, [jnp.max(s, axis=0, keepdims=True) for s in scores])
        top = top * factor
        mixed = None
        for i in range(count):
            probs = jnp.exp2(scores[i] * factor - top).astype(BF)
            value = jnp.where(keep, v_refs[i][...], jnp.ones((), BF))
            part = mm_rows(value, probs)
            mixed = part if mixed is None else mixed + part
        if head == 0:
            total, mixed = mixed[HD : HD + 1], mixed[:HD]
        else:
            total, mixed = mixed[:1], mixed[HD:]
        outs.append(mixed / total)
        lse_ref[0, head : head + 1, :] = top + jnp.log2(total)
    o_ref[...] = jnp.concatenate(outs, 0).T.astype(BF)


def attend(query, keyed, mask, begin=0, pairs=None, into=None):
    rows, model = query.shape
    count, every = len(keyed), model // 128
    pairs = every if pairs is None else pairs
    at = lambda base: pl.BlockSpec((rows, 128), lambda j: (0, base + begin + j))
    earlier = [] if into is None else list(into)

    def kernel(*refs):
        inputs = 2 + 2 * count
        attend_kernel(count, HD**-0.5, *refs[:inputs], *refs[inputs + len(earlier) :])

    return pl.pallas_call(
        kernel,
        grid=(pairs,),
        in_specs=[at(0), pl.BlockSpec((count, rows, 128), lambda j: (0, 0, 0))]
        + [at(0)] * count
        + [at(every)] * count
        + [pl.BlockSpec(memory_space=pl.ANY)] * len(earlier),
        out_specs=[at(0), pl.BlockSpec((1, 8, rows), lambda j: (begin + j, 0, 0))],
        out_shape=[
            jax.ShapeDtypeStruct((rows, model), BF),
            jax.ShapeDtypeStruct((every, 8, rows), F32),
        ],
        input_output_aliases={2 + 2 * count + i: i for i in range(len(earlier))},
        compiler_params=pltpu.CompilerParams(vmem_limit_bytes=56 << 20),
        name="attend",
    )(query, mask, *keyed, *keyed, *earlier)


def attend_back_kernel(count, scale, q_ref, do_ref, o_ref, lse_ref, mask_ref, *refs):
    k_refs, v_refs = refs[:count], refs[count : 2 * count]
    dq_ref = refs[2 * count]
    dkv_refs = refs[2 * count + 1 :]
    rows = q_ref.shape[0]
    factor = scale * LOG2E
    lane = lanes((rows, 128))
    first = lane < HD
    one = jnp.where(lane % HD == 0, 1.0, 0.0).astype(BF)
    two = jnp.where(lane % HD < 2, 1.0, 0.0).astype(BF)
    wide = do_ref[...].astype(F32)
    product = wide * o_ref[...].astype(F32)
    d_query = []
    keeps = (first, jnp.logical_not(first))
    d_key = [[None] * 2 for _ in range(count)]
    d_value = [[None] * 2 for _ in range(count)]
    for head in range(2):
        keep = keeps[head]
        query = jnp.where(keep, q_ref[...], one)
        delta = jnp.sum(jnp.where(keep, product, 0.0), axis=1, keepdims=True)
        high = delta.astype(BF).astype(F32)
        spare = lane % HD
        extra = jnp.where(spare == 0, -high, jnp.where(spare == 1, high - delta, 0.0))
        d_out = jnp.where(keep, wide, extra).astype(BF)
        lse = lse_ref[0, head : head + 1, :]
        grad = None
        for i in range(count):
            key = jnp.where(keep, k_refs[i][...], mask_ref[i])
            scores = mm_back(key, query)
            probs = jnp.exp2(scores * factor - lse)
            d_probs = mm_back(jnp.where(keep, v_refs[i][...], two), d_out)
            d_scores = (probs * d_probs).astype(BF)
            d_value[i][head] = mm(probs.astype(BF), do_ref[...])
            d_key[i][head] = mm(d_scores, query)
            part = mm_rows(k_refs[i][...], d_scores)
            grad = part if grad is None else grad + part
        d_query.append(grad[:HD] if head == 0 else grad[HD:])
    dq_ref[...] = (jnp.concatenate(d_query, 0).T * scale).astype(BF)
    for i in range(count):
        dkv_refs[i][0] = (jnp.where(first, *d_key[i]) * scale).astype(BF)
        dkv_refs[i][1] = jnp.where(first, *d_value[i]).astype(BF)


def attend_back(query, d_mixed, mixed, lse, keyed, mask, begin, pairs):
    rows, model = query.shape
    count, every = len(keyed), model // 128
    at = lambda base: pl.BlockSpec((rows, 128), lambda j: (0, base + begin + j))
    outs = pl.pallas_call(
        functools.partial(attend_back_kernel, count, HD**-0.5),
        grid=(pairs,),
        in_specs=[at(0)] * 3
        + [pl.BlockSpec((1, 8, rows), lambda j: (begin + j, 0, 0))]
        + [pl.BlockSpec((count, rows, 128), lambda j: (0, 0, 0))]
        + [at(0)] * count
        + [at(every)] * count,
        out_specs=[pl.BlockSpec((rows, 128), lambda j: (0, j))]
        + [pl.BlockSpec((2, rows, 128), lambda j: (0, 0, j))] * count,
        out_shape=[jax.ShapeDtypeStruct((rows, pairs * 128), BF)]
        + [jax.ShapeDtypeStruct((2, rows, pairs * 128), BF)] * count,
        compiler_params=pltpu.CompilerParams(vmem_limit_bytes=56 << 20),
        name="attend_back",
    )(query, d_mixed, mixed, lse, mask, *keyed, *keyed)
    return outs[0], list(outs[1:])


def forward_layer(grid, group_bits, hidden, params, mask, hooks=None):
    flat_low = hidden.astype(BF)
    keyed = (mm(flat_low, params["kv"]) + params["kv_bias"]).astype(BF)
    pieces = [keyed]
    for bit in group_bits:
        pieces = pieces + [grid.flip(v, bit) for v in pieces]
    query = (mm(flat_low, params["q"]) + params["q_bias"]).astype(BF)
    if hooks is None:
        mixed, lse = attend(query, pieces, mask)
    else:
        pairs = query.shape[1] // 128
        part = attend(query, pieces, mask, 0, pairs // 2)
        query, part, waiting = hooks[0](query, part)
        mixed, lse = attend(query, pieces, mask, pairs // 2, pairs - pairs // 2, part)
        mixed, more, waiting = hooks[1](mixed, waiting)
        params.update(more)
    joined = hidden + mm(mixed, params["out"]) + params["out_bias"]
    first = normalize(joined, params["first_gain"], params["first_shift"])
    first_low = first.astype(BF)
    if hooks is not None:
        first_low, waiting = hooks[2](first_low, waiting)
    inner = mm(first_low, params["up"]) + params["up_bias"]
    act_low = activate(inner).astype(BF)
    if hooks is not None:
        act_low, more = hooks[3](act_low, waiting)
        params.update(more)
    summed = first + mm(act_low, params["down"]) + params["down_bias"]
    result = normalize(summed, params["second_gain"], params["second_shift"])
    return result, (flat_low, query, pieces, mixed, lse, joined, first_low, inner, act_low, summed)


class Backward:
    def __init__(self, grid, group_bits, saved, params, mask):
        self.grid, self.group_bits, self.params, self.mask = grid, group_bits, params, mask
        (
            self.flat_low,
            self.query,
            self.pieces,
            self.mixed,
            self.lse,
            self.joined,
            self.first_low,
            self.inner,
            self.act_low,
            self.summed,
        ) = saved

    def top(self, grad_out):
        p = self.params
        _, back = jax.vjp(normalize, self.summed, p["second_gain"], p["second_shift"])
        self.d_summed, self.d_second_gain, self.d_second_shift = back(grad_out)
        self.d_down = self.d_summed.astype(BF)

    def hidden_units(self):
        d_act = mm_back(self.d_down, self.params["down"])
        _, act_back = jax.vjp(activate, self.inner)
        self.d_inner = act_back(d_act)[0].astype(BF)

    def middle(self):
        p = self.params
        d_first = self.d_summed + mm_back(self.d_inner, p["up"])
        _, back = jax.vjp(normalize, self.joined, p["first_gain"], p["first_shift"])
        self.d_joined, self.d_first_gain, self.d_first_shift = back(d_first)
        self.d_branch = self.d_joined.astype(BF)

    def attention(self, begin, pairs):
        d_query, d_keyed = attend_back(
            self.query, self.d_mixed, self.mixed, self.lse, self.pieces, self.mask, begin, pairs
        )
        for bit in reversed(self.group_bits):
            half = len(d_keyed) // 2
            sent = [self.grid.flip(v, bit) for v in d_keyed[half:]]
            d_keyed = [
                (mine.astype(F32) + got.astype(F32)).astype(BF)
                for mine, got in zip(d_keyed[:half], sent)
            ]
        return d_query, d_keyed[0]

    def collect(self, parts):
        self.d_query = side_by_side([q for q, _ in parts], 1)
        self.d_keyed = jnp.concatenate([kv[i] for i in range(2) for _, kv in parts], 1)

    def start(self):
        return (
            self.d_joined
            + mm_back(self.d_query, self.params["q"])
            + mm_back(self.d_keyed, self.params["kv"])
        )

    def vectors(self):
        model = self.d_query.shape[1]
        rows = (
            column_sum(self.d_query),
            column_sum(self.d_keyed[:, model:]),
            column_sum(self.d_branch),
            self.d_first_gain,
            self.d_first_shift,
            column_sum(self.d_down),
            self.d_second_gain,
            self.d_second_shift,
        )
        return rows, column_sum(self.d_inner)


def local(n_dp, n_ctx, tokens, lengths, teacher, *shards):
    (
        query_weight,
        query_bias,
        key_weight,
        value_weight,
        value_bias,
        out_weight,
        out_bias,
        first_gain,
        first_shift,
        up_weight,
        up_bias,
        down_weight,
        down_bias,
        second_gain,
        second_shift,
    ) = shards
    grid = Grid(n_dp, n_ctx)
    width, seqs, model = tokens.shape
    inner_width = up_weight.shape[1]
    rows = query_weight.shape[0]
    block = rows * n_ctx

    spread = n_ctx // (2 * seqs)
    mine = grid.ctx // spread
    member = grid.core * spread + grid.ctx % spread
    group_bits = [1 << i for i in range(spread.bit_length() - 1)] + [grid.core_bit]

    def route(turn):
        pairs = []
        for pair in range(n_dp // 2):
            for core in range(2):
                for at in range(n_ctx):
                    seq = core * seqs + (at + turn) % seqs
                    to = at // seqs
                    there = (pair * 2 + to // spread) * n_ctx + seq * spread + to % spread
                    pairs.append(((pair * 2 + core) * n_ctx + at, there))
        return pairs

    def to_group(values, turn):
        value = lax.dynamic_index_in_dim(values, (grid.ctx + turn) % seqs, 1, keepdims=False)
        return lax.ppermute(value, AXES, route(turn))

    def to_groups(values):
        return jnp.concatenate([to_group(values, turn) for turn in range(seqs)], 0)

    def send_back(values):
        return [
            lax.ppermute(
                values[turn * width : (turn + 1) * width],
                AXES,
                [(there, here) for here, there in route(turn)],
            )
            for turn in range(seqs)
        ]

    def put_back(got):
        return jnp.stack(
            [
                functools.reduce(
                    lambda a, t: jnp.where((grid.ctx + t) % seqs == seq, got[t], a),
                    range(1, seqs),
                    got[0],
                )
                for seq in range(seqs)
            ],
            1,
        )

    turns = list(reversed(grid.ctx_bits))
    vectors = (
        query_bias,
        value_bias,
        out_bias,
        first_gain,
        first_shift,
        down_bias,
        second_gain,
        second_shift,
    )
    one = [jnp.concatenate([query_weight, key_weight, value_weight], 1)]
    small = [
        jnp.concatenate(
            [jnp.stack(vectors, 0).T, up_bias.reshape(rows, -1), jnp.zeros((rows, 116), BF)], 1
        )
    ]
    two, three = [jnp.concatenate([out_weight, up_weight], 1)], [down_weight]
    last = len(turns) - 1
    got_two = None
    for i, turn in enumerate(turns):
        got = [grid.flip(side_by_side(v), turn) for v in (one, small)]
        if got_two is not None:
            two = join_ctx(grid, two, got_two, turns[i - 2])
        got_two = grid.flip(side_by_side(two), turns[i - 1]) if i else None
        got, got_two, two, tokens = meet(got, got_two, two, tokens)
        one, small = join_ctx(grid, one, got[0], turn), join_ctx(grid, small, got[1], turn)
    if got_two is not None:
        two = join_ctx(grid, two, got_two, turns[last - 1])
    first = Gather(grid, jnp.concatenate([side_by_side(one), side_by_side(small)], 1))
    got, start, two, tokens = meet(
        first.first(), [to_group(tokens, turn) for turn in range(seqs - 1)], two, tokens
    )
    more, crossed = first.second(*got)
    got_two = grid.flip(side_by_side(two), turns[last])
    more, crossed, start, got_two, two, three = meet(
        more, crossed, start + [to_group(tokens, seqs - 1)], got_two, two, three
    )
    second = Gather(grid, side_by_side(join_ctx(grid, two, got_two, turns[last])))
    second_got = second.first()
    for turn in turns[:-1]:
        three = join_ctx(grid, three, grid.flip(side_by_side(three), turn), turn)
    start = jnp.concatenate(start, 0)
    whole_q, whole_kv, whole_small = assemble(
        grid,
        first.finish(more, crossed),
        block,
        [
            (0, model, 0, 0, block, 0),
            (model, 2 * model, 1, 0, block, 0),
            (3 * model, 128, 2, 0, block, 0),
        ],
        [(model, model), (model, 2 * model), (model, 128)],
    )
    flat_small = whole_small[:, :12].astype(F32)
    by_vector = flat_small[:, :8].T
    params = {
        "q": whole_q,
        "kv": whole_kv,
        "q_bias": by_vector[0],
        "kv_bias": jnp.concatenate([jnp.zeros((model,), F32), by_vector[1]]),
        "out_bias": by_vector[2],
        "first_gain": by_vector[3],
        "first_shift": by_vector[4],
        "down_bias": by_vector[5],
        "second_gain": by_vector[6],
        "second_shift": by_vector[7],
        "up_bias": flat_small[:, 8:12].reshape(inner_width),
    }

    theirs = grid.flip(lengths, grid.core_bit)
    length = jnp.where(mine // seqs == grid.core, lengths[mine % seqs], theirs[mine % seqs])

    def slots_of(who):
        place = jnp.arange(width, dtype=jnp.int32)
        return jnp.concatenate(
            [width * (seqs * who + (mine + turn) % seqs) + place for turn in range(seqs)]
        )

    live = (slots_of(member) < length).astype(F32)[:, None]
    relative = [0]
    for bit in group_bits:
        relative = relative + [r ^ (spread if bit == grid.core_bit else bit) for r in relative]
    excluded = jnp.stack([jnp.where(slots_of(member ^ r) < length, 0.0, MASKED) for r in relative])
    mask = jnp.where(jnp.arange(128) % HD == 0, excluded[:, :, None], 0.0).astype(BF)

    def middle_of_attention(query, part):
        query, part, got, parts = meet(query, part, second_got, three)
        state = second.second(*got)
        return query, part, (state, parts, grid.flip(side_by_side(parts), turns[last]))

    def after_attention(mixed, waiting):
        mixed, (more, crossed), parts, got = meet(mixed, *waiting)
        third = Gather(grid, side_by_side(join_ctx(grid, parts, got, turns[last])))
        got = third.first()
        whole_out, whole_up = assemble(
            grid,
            second.finish(more, crossed),
            block,
            [(0, model, 0, 0, block, 0), (model, inner_width, 1, 0, block, 0)],
            [(model, model), (model, inner_width)],
        )
        return mixed, {"out": whole_out, "up": whole_up}, (third, got)

    def before_up(first_low, waiting):
        third, got = waiting
        first_low, got = meet(first_low, got)
        return first_low, (third, third.second(*got))

    def after_up(act_low, waiting):
        third, state = waiting
        act_low, (more, crossed) = meet(act_low, state)
        tall = third.part.shape[0]
        (whole_down,) = assemble(
            grid,
            third.finish(more, crossed),
            tall,
            [(0, model, 0, 0, tall, 0)],
            [(inner_width, model)],
        )
        return act_low, {"down": whole_down}

    hooks = (middle_of_attention, after_attention, before_up, after_up)
    middle, first_saved = forward_layer(
        grid, group_bits, start.astype(F32), params, mask, hooks
    )
    target = to_groups(after(teacher, middle))
    result, second_saved = forward_layer(grid, group_bits, middle, params, mask)
    layer_got = send_back(result.astype(BF))
    diff = (result - target.astype(F32)) * live
    error = jnp.sum(diff * diff)

    pairs = model // 128
    b = Backward(grid, group_bits, second_saved, params, mask)
    b.top(diff)
    b.hidden_units()
    b.middle()
    b.d_mixed = mm_back(b.d_branch, params["out"]).astype(BF)
    b.collect([b.attention(0, pairs)])
    d_middle = b.start()

    a = Backward(grid, group_bits, first_saved, params, mask)
    a.top(d_middle)
    downs = grads(grid, [b.act_low, a.act_low], [b.d_down, a.d_down])
    downs, layer_got = meet(downs, layer_got)
    layer_out = put_back(layer_got)
    reduce_down, reduce_up, reduce_rest = Reduce(grid), Reduce(grid), Reduce(grid)
    reduce_down.add(*downs)
    a.d_down = after(a.d_down, downs)
    a.hidden_units()
    ups = grads(grid, [b.first_low, a.first_low], [b.d_inner, a.d_inner])
    reduce_up.add(*ups)
    reduce_down.first(ups)
    a.d_inner = after(a.d_inner, ups)
    a.middle()
    outs = grads(grid, [b.mixed, a.mixed], [b.d_branch, a.d_branch])
    reduce_up.add(*outs)
    a.d_mixed = mm_back(after(a.d_branch, outs, reduce_down.sent()), params["out"]).astype(BF)
    part_one = a.attention(0, pairs // 2)
    reduce_down.second(part_one[0])
    reduce_up.first(part_one[0])
    a.d_mixed = after(a.d_mixed, part_one, reduce_down.sent(), reduce_up.sent())
    reduce_down.third(reduce_up.halves)
    part_two = a.attention(pairs // 2, pairs - pairs // 2)
    a.collect([part_one, part_two])
    lefts = [b.flat_low, a.flat_low]
    rest_q = grads(grid, lefts, [b.d_query, a.d_query])
    reduce_rest.add(*rest_q)
    reduce_up.second(rest_q)
    rest_kv = grads(grid, lefts, [b.d_keyed, a.d_keyed])
    reduce_rest.add(*rest_kv)
    reduce_down.fourth(rest_kv)
    rows_b, wide_b = b.vectors()
    rows_a, wide_a = a.vectors()
    stacked = (jnp.concatenate(rows_b) + jnp.concatenate(rows_a)).reshape(8, model)
    number = jnp.sum(live)
    whole = [(v, v.astype(BF).astype(F32)) for v in (error, number)]
    here = (jnp.arange(grid.n) == grid.lin)[None, :]
    marks = [jnp.where(here, v, 0.0) for full, low in whole for v in (low, full - low)]
    spare = -(12 + 4 * grid.n) % 128
    marks = jnp.concatenate(marks + [jnp.zeros((1, spare), F32)], 1)
    small = jnp.concatenate(
        [
            stacked.T,
            (wide_b + wide_a).reshape(model, -1),
            jnp.broadcast_to(marks, (model, marks.shape[1])),
        ],
        1,
    ).reshape(n_dp // 2, 2, block, -1)
    pick = functools.partial(lax.dynamic_index_in_dim, axis=1, keepdims=False)
    reduce_rest.add(pick(small, 1 - grid.core).astype(BF), pick(small, grid.core))
    a.d_query = after(a.d_query, rest_kv)
    d_start = a.start()
    grad_tokens = put_back(send_back(d_start.astype(BF)))
    reduce_rest.first(d_start)
    reduce_up.third(reduce_rest.sent())
    reduce_rest.second()
    reduce_up.fourth(reduce_rest.sent())
    reduce_rest.third()
    grad_down = reduce_down.finish_value()
    grad_out_up = reduce_up.finish_value()
    grad_rest = reduce_rest.finish_value()
    grad_small = grad_rest[:, 3 * model :]
    sums = jnp.sum(grad_small[:1, 12 : 12 + 4 * grid.n].reshape(4, grid.n), axis=1)
    loss = (sums[0] + sums[1]) / ((sums[2] + sums[3]) * model)
    vector = [grad_small[:, i] for i in range(8)]
    return (
        layer_out,
        loss,
        grad_tokens,
        grad_rest[:, :model],
        vector[0],
        grad_rest[:, model : 2 * model],
        grad_rest[:, 2 * model : 3 * model],
        vector[1],
        grad_out_up[:, inner_width:],
        vector[2],
        vector[3],
        vector[4],
        grad_out_up[:, :inner_width],
        grad_small[:, 8:12].reshape(-1),
        grad_down,
        vector[5],
        vector[6],
        vector[7],
    )


def solution(mesh):
    matrix, vector = P(AXES, None), P(AXES)
    states = P("ctx", "dp", None)
    params = (
        matrix,
        vector,
        matrix,
        matrix,
        vector,
        matrix,
        vector,
        vector,
        vector,
        matrix,
        vector,
        matrix,
        vector,
        vector,
        vector,
    )
    return jax.shard_map(
        functools.partial(local, mesh.shape["dp"], mesh.shape["ctx"]),
        mesh=mesh,
        in_specs=(states, P("dp"), states) + params,
        out_specs=(states, P(), states) + params,
        check_vma=False,
    )
```
